256 devices in a mesh: segment: 2 (over core), et: 128 (over x, y, z).
Axes of the slice: x: 4, y: 4, z: 8, core: 2. Of those that a mesh axis runs over, the one named last changes fastest.
Arguments:
- inputs: bfloat16 [1, 128, 6144], P(None, 'et'), may hold values from -6 to 6
- cotangent: bfloat16 [1, 128, 6144], P(None, 'et'), may hold values from -6 to 6
- gate_weight: bfloat16 [2, 6144, 16384], P('segment', None, 'et'), may hold values from -0.078125 to 0.078125
- up_weight: bfloat16 [2, 6144, 16384], P('segment', None, 'et'), may hold values from -0.078125 to 0.078125
- down_weight: bfloat16 [2, 16384, 6144], P('segment', 'et'), may hold values from -0.0625 to 0.0625
- route_rows: int32 [2, 1, 128], P('segment'), may hold values from 0 to 127, as said below
- route_count: int32 [2, 1], P('segment'), may hold values from 32 to 128, as said below
- route_weight: float32 [2, 1, 128], P('segment'), may hold values from 0.05 to 1
- width_mask: int32 [2, 128], P('segment', 'et'), may hold values from 0 to 1, as said below
Outputs:
- section_output: bfloat16 [2, 1, 128, 6144], P('segment', None, 'et')
- grad_input: bfloat16 [2, 1, 128, 6144], P('segment', None, 'et')
- grad_gate: bfloat16 [2, 6144, 16384], P('segment', None, 'et')
- grad_up: bfloat16 [2, 6144, 16384], P('segment', None, 'et')
- grad_down: bfloat16 [2, 16384, 6144], P('segment', 'et')
The draws below stay inside these ranges and needn't reach their ends.
Inputs may be any that keep to these rules, and one draw needn't show every extreme that they name: `route_rows`: each list names every one of the 128 tokens once; its first route_count entries are the slots routed to the expert. `route_count`: 128 in at least one entry. `width_mask`: the kept tiles of each section are its first ones, at least 32 of them and never all.
All inputs are finite; a program needn't handle non-finite values.
Results may differ from the reference program's by a relative error of at most 0.015.
Values may be sent and summed in bfloat16 or wider, within the bound.
No kernel may reach another device: no remote copies, remote signals or barrier semaphores. Data moves between devices by JAX's collectives and lax.ppermute only.
A program may use at most 128 MiB of HBM per device.

```python
import math
import jax
import jax.numpy as jnp
from jax import lax

D = 6144
FF = 16384
TILE = 128
MICRO = 1
SEGMENTS = 2
TOKENS = 128
SLOTS = 128
TILES = 128


def draw_route_rows(key, part):
    keys = jax.random.split(jax.random.fold_in(key, 11), SEGMENTS * MICRO)
    orders = jax.vmap(lambda single: jax.random.permutation(single, SLOTS))(keys)
    return orders.astype(jnp.int32).reshape(SEGMENTS, MICRO, SLOTS)


def draw_route_count(key, part):
    first_key = jax.random.fold_in(key, 21)
    second_key = jax.random.fold_in(key, 22)
    counts = jax.random.randint(first_key, (SEGMENTS * MICRO,), SLOTS // 4, SLOTS + 1).astype(jnp.int32)
    chosen = jax.random.randint(second_key, (), 0, SEGMENTS * MICRO).astype(jnp.int32)
    counts = counts.at[chosen].set(SLOTS)
    return counts.reshape(SEGMENTS, MICRO)


def draw_width_mask(key, part):
    widths = jax.random.randint(jax.random.fold_in(key, 31), (SEGMENTS, 1), TILES // 4, TILES).astype(jnp.int32)
    return (jnp.arange(TILES, dtype=jnp.int32)[None, :] < widths).astype(jnp.int32)


def steps_of(rng, shape, shards, low, top_value):
    loudness, own = 1.0, jax.random.fold_in(rng, 6)
    for dim, parts in shards:
        steps = jnp.exp(jax.random.uniform(jax.random.fold_in(own, dim), (parts,), jnp.float32, low / len(shards), top_value / len(shards)))
        loudness = loudness * jnp.repeat(steps, shape[dim] // parts).reshape([-1 if axis == dim else 1 for axis in range(len(shape))])
    return loudness


def gaussian(stream_key, extent, scale, reach, pieces=(), held_as=jnp.bfloat16):
    values = jax.random.normal(stream_key, extent, jnp.float32) * scale
    if len(pieces) > 0:
        values = steps_of(stream_key, extent, pieces, -0.22, 0.18) * values
    return jnp.clip(values, min=-reach, max=reach).astype(held_as)


def setup_inputs(seed: int = 0) -> dict:
    seeds = jax.random.split(jax.random.key(seed), 10)
    inputs = gaussian(seeds[0], (MICRO, TOKENS, D), 1.0, 6.0, ((1, 128),))
    cotangent = gaussian(seeds[1], (MICRO, TOKENS, D), 1.0, 6.0, ((1, 128),))
    gate_weight = gaussian(seeds[2], (SEGMENTS, D, FF), D ** -0.5, 0.078125, ((0, 2), (2, 128)))
    up_weight = gaussian(seeds[3], (SEGMENTS, D, FF), D ** -0.5, 0.078125, ((0, 2), (2, 128)))
    down_weight = gaussian(seeds[4], (SEGMENTS, FF, D), (FF // 2) ** -0.5, 0.0625, ((0, 2), (1, 128)))
    route_rows = draw_route_rows(jax.random.fold_in(seeds[9], 71), 0)
    route_count = draw_route_count(jax.random.fold_in(seeds[9], 71), 0)
    route_weight = jnp.clip(jnp.exp(math.log(1.0) - 2.9957323 * jax.random.uniform(seeds[7], (SEGMENTS, MICRO, SLOTS), jnp.float32) ** steps_of(seeds[7], (SEGMENTS, MICRO, SLOTS), ((0, 2),), -0.2, 0.2)), 0.05, 1.0)
    width_mask = draw_width_mask(jax.random.fold_in(seeds[9], 71), 0)
    return dict(inputs=inputs, cotangent=cotangent, gate_weight=gate_weight, up_weight=up_weight, down_weight=down_weight, route_rows=route_rows, route_count=route_count, route_weight=route_weight, width_mask=width_mask)


def expert_forward(picked, gate_w, up_w, down_w, keep):
    gate_value = jnp.dot(picked, gate_w, preferred_element_type=jnp.float32)
    up_value = jnp.dot(picked, up_w, preferred_element_type=jnp.float32)
    hidden = (gate_value * jax.nn.sigmoid(gate_value) * up_value * keep).astype(jnp.bfloat16)
    outcome = jnp.dot(hidden, down_w, preferred_element_type=jnp.float32)
    return gate_value, up_value, hidden, outcome


def expert_backward(picked, slot_grad_in, gate_value, up_value, hidden, gate_w, up_w, down_w, keep):
    contract_last = (((1,), (1,)), ((), ()))
    contract_first = (((0,), (0,)), ((), ()))
    hidden_delta = lax.dot_general(slot_grad_in, down_w, contract_last, preferred_element_type=jnp.float32)
    sig_gate = jax.nn.sigmoid(gate_value)
    gate_delta = (hidden_delta * keep * up_value * sig_gate * (1.0 + gate_value * (1.0 - sig_gate))).astype(jnp.bfloat16)
    up_delta = (hidden_delta * keep * gate_value * sig_gate).astype(jnp.bfloat16)
    grad_gate = lax.dot_general(picked, gate_delta, contract_first, preferred_element_type=jnp.float32)
    grad_up = lax.dot_general(picked, up_delta, contract_first, preferred_element_type=jnp.float32)
    grad_down = lax.dot_general(hidden, slot_grad_in, contract_first, preferred_element_type=jnp.float32)
    slot_grad = lax.dot_general(gate_delta, gate_w, contract_last, preferred_element_type=jnp.float32)
    slot_grad = slot_grad + lax.dot_general(up_delta, up_w, contract_last, preferred_element_type=jnp.float32)
    return grad_gate, grad_up, grad_down, slot_grad


def reference(inputs, cotangent, gate_weight, up_weight, down_weight, route_rows, route_count, route_weight, width_mask):
    slot_index = jnp.arange(SLOTS, dtype=jnp.int32)
    keeps = [jnp.repeat(width_mask[s].astype(jnp.float32), TILE) for s in range(SEGMENTS)]
    current = [inputs[m] for m in range(MICRO)]
    saved = []
    outputs = []
    for s in range(SEGMENTS):
        saved_segment = []
        results = []
        for m in range(MICRO):
            slot_rows = route_rows[s, m]
            scale = jnp.where(slot_index < route_count[s, m], route_weight[s, m], 0.0)
            picked = current[m][slot_rows]
            gate_value, up_value, hidden, outcome = expert_forward(picked, gate_weight[s], up_weight[s], down_weight[s], keeps[s])
            added = jnp.zeros((TOKENS, D), jnp.float32).at[slot_rows].add(scale[:, None] * outcome)
            results.append((current[m].astype(jnp.float32) + added).astype(jnp.bfloat16))
            saved_segment.append((picked, gate_value, up_value, hidden, scale))
        saved.append(saved_segment)
        outputs.append(jnp.stack(results))
        current = results
    upstream = [cotangent[m] for m in range(MICRO)]
    grad_inputs = [None] * SEGMENTS
    grads_gate = [None] * SEGMENTS
    grads_up = [None] * SEGMENTS
    grads_down = [None] * SEGMENTS
    for s in reversed(range(SEGMENTS)):
        acc_gate = jnp.zeros((D, FF), jnp.float32)
        acc_up = jnp.zeros((D, FF), jnp.float32)
        acc_down = jnp.zeros((FF, D), jnp.float32)
        results = []
        for m in range(MICRO):
            picked, gate_value, up_value, hidden, scale = saved[s][m]
            slot_rows = route_rows[s, m]
            slot_grad_in = (scale[:, None] * upstream[m][slot_rows].astype(jnp.float32)).astype(jnp.bfloat16)
            part_gate, part_up, part_down, slot_grad = expert_backward(picked, slot_grad_in, gate_value, up_value, hidden, gate_weight[s], up_weight[s], down_weight[s], keeps[s])
            acc_gate = acc_gate + part_gate
            acc_up = acc_up + part_up
            acc_down = acc_down + part_down
            added = jnp.zeros((TOKENS, D), jnp.float32).at[slot_rows].add(slot_grad)
            results.append((upstream[m].astype(jnp.float32) + added).astype(jnp.bfloat16))
        grad_inputs[s] = jnp.stack(results)
        grads_gate[s] = acc_gate.astype(jnp.bfloat16)
        grads_up[s] = acc_up.astype(jnp.bfloat16)
        grads_down[s] = acc_down.astype(jnp.bfloat16)
        upstream = results
    return (jnp.stack(outputs), jnp.stack(grad_inputs), jnp.stack(grads_gate), jnp.stack(grads_up), jnp.stack(grads_down))
```

```python
import jax
import jax.numpy as jnp
from jax import lax
from jax.sharding import PartitionSpec as P

LANES = 128
CONTRACT_LAST = (((1,), (1,)), ((), ()))
CONTRACT_FIRST = (((0,), (0,)), ((), ()))


def exchange(value):
    return lax.all_to_all(value, "et", 0, 0, tiled=True)


def spread(row):
    size = lax.axis_size("et")
    return exchange(jnp.broadcast_to(row[None], (size, *row.shape)))


def collect(parts):
    size = lax.axis_size("et")
    tiles = parts.reshape(size, -1, LANES).astype(jnp.bfloat16)
    return jnp.sum(exchange(tiles).astype(jnp.float32), axis=0)


def across(value, pairs):
    return lax.ppermute(value, "segment", pairs)


def dot_f32(a, b):
    return jnp.dot(a, b, preferred_element_type=jnp.float32)


def per_device(
    inputs,
    cotangent,
    gate_weight,
    up_weight,
    down_weight,
    route_rows,
    route_count,
    route_weight,
    width_mask,
):
    width = inputs.shape[2]
    half = width // 2
    tokens = lax.axis_size("et")
    first = lax.axis_index("segment") == 0
    gate_w = gate_weight[0]
    up_w = up_weight[0]
    down_w = down_weight[0]
    keep = width_mask[0, 0].astype(jnp.float32)
    to_one, to_zero, both = [(0, 1)], [(1, 0)], [(0, 1), (1, 0)]

    slots = route_rows.shape[2]
    live = jnp.arange(slots, dtype=jnp.int32) < route_count[0, 0]
    slot_scale = jnp.where(live, route_weight[0, 0], 0.0)
    chosen = route_rows[0, 0][None, :] == jnp.arange(tokens, dtype=jnp.int32)[:, None]
    scale = jnp.sum(jnp.where(chosen, slot_scale[None, :], 0.0), axis=1, keepdims=True)

    in_rows = inputs[0].reshape(2, half // LANES, LANES)
    in_half = jnp.where(first, in_rows[0], in_rows[1])
    cot_rows = cotangent[0].reshape(2, half // LANES, LANES)
    cot_half = jnp.where(first, cot_rows[0], cot_rows[1])
    cot_all = lax.all_gather(cotangent[0], "et", axis=0, tiled=True)

    mine = spread(in_half).reshape(tokens, half)
    tokens_in = jnp.concatenate([mine, across(mine, to_zero)], axis=1)
    gate_value = dot_f32(tokens_in, gate_w)
    up_value = dot_f32(tokens_in, up_w)
    hidden = (gate_value * jax.nn.sigmoid(gate_value) * up_value * keep).astype(jnp.bfloat16)
    outcome = (scale * dot_f32(hidden, down_w)).astype(jnp.bfloat16)
    other = across(outcome[:, half:], to_one)
    total = collect(jnp.where(first, outcome[:, :half], other))
    mid_half = (in_half.astype(jnp.float32) + total).astype(jnp.bfloat16)
    mine = spread(mid_half).reshape(tokens, half)
    tokens_mid = jnp.concatenate([across(mine, to_one), mine], axis=1)
    picked = jnp.where(first, tokens_in, tokens_mid)

    gate_value = dot_f32(picked, gate_w)
    up_value = dot_f32(picked, up_w)
    sig = jax.nn.sigmoid(gate_value)
    hidden = (gate_value * sig * up_value * keep).astype(jnp.bfloat16)
    outcome = (scale * dot_f32(hidden, down_w)).astype(jnp.bfloat16)
    gate_slope = keep * up_value * sig * (1.0 + gate_value * (1.0 - sig))
    up_slope = keep * gate_value * sig

    def backward(upstream):
        slot_grad_in = (scale * upstream.astype(jnp.float32)).astype(jnp.bfloat16)
        hidden_delta = lax.dot_general(
            slot_grad_in, down_w, CONTRACT_LAST, preferred_element_type=jnp.float32
        )
        gate_delta = (hidden_delta * gate_slope).astype(jnp.bfloat16)
        up_delta = (hidden_delta * up_slope).astype(jnp.bfloat16)
        slot_grad = lax.dot_general(
            gate_delta, gate_w, CONTRACT_LAST, preferred_element_type=jnp.float32
        ) + lax.dot_general(up_delta, up_w, CONTRACT_LAST, preferred_element_type=jnp.float32)
        return slot_grad_in, gate_delta, up_delta, slot_grad.astype(jnp.bfloat16)

    _, _, _, slot_grad = backward(cot_all)
    other = across(slot_grad[:, :half], to_zero)
    total = collect(jnp.where(first, other, slot_grad[:, half:]))
    back_half = (cot_half.astype(jnp.float32) + total).astype(jnp.bfloat16)
    mine = spread(back_half).reshape(tokens, half)
    back_all = jnp.concatenate([mine, across(mine, to_zero)], axis=1)
    upstream = jnp.where(first, back_all, cot_all)

    slot_grad_in, gate_delta, up_delta, slot_grad = backward(upstream)
    total = collect(jnp.where(first, slot_grad, outcome))

    def whole(piece):
        other_piece = across(piece, both)
        low = jnp.where(first, piece, other_piece)
        high = jnp.where(first, other_piece, piece)
        return jnp.concatenate([low, high], axis=0)

    mid_row = whole(mid_half)
    back_row = whole(back_half)
    last = (jnp.where(first, back_row, mid_row).astype(jnp.float32) + total).astype(jnp.bfloat16)
    section_output = jnp.where(first, mid_row, last)
    grad_input = jnp.where(first, last, back_row)

    grad_gate = lax.dot_general(
        picked, gate_delta, CONTRACT_FIRST, preferred_element_type=jnp.float32
    )
    grad_up = lax.dot_general(picked, up_delta, CONTRACT_FIRST, preferred_element_type=jnp.float32)
    grad_down = lax.dot_general(
        hidden, slot_grad_in, CONTRACT_FIRST, preferred_element_type=jnp.float32
    )
    return (
        section_output.reshape(1, 1, 1, width),
        grad_input.reshape(1, 1, 1, width),
        grad_gate.astype(jnp.bfloat16)[None],
        grad_up.astype(jnp.bfloat16)[None],
        grad_down.astype(jnp.bfloat16)[None],
    )


def solution(mesh):
    return jax.shard_map(
        per_device,
        mesh=mesh,
        in_specs=(
            P(None, "et", None),
            P(None, "et", None),
            P("segment", None, "et"),
            P("segment", None, "et"),
            P("segment", "et", None),
            P("segment", None, None),
            P("segment", None),
            P("segment", None, None),
            P("segment", "et"),
        ),
        out_specs=(
            P("segment", None, "et", None),
            P("segment", None, "et", None),
            P("segment", None, "et"),
            P("segment", None, "et"),
            P("segment", "et", None),
        ),
        check_vma=False,
    )
```

```python
import jax
import jax.numpy as jnp
from jax import lax
from jax.sharding import Mesh
from jax.sharding import PartitionSpec as P

LANES = 128
PLANE = ("x", "y")
LINE = "z"
ET = ("x", "y", "z")
SIZES = (4, 4, 8)
CONTRACT_LAST = (((1,), (1,)), ((), ()))
CONTRACT_FIRST = (((0,), (0,)), ((), ()))


def exchange(value, axes):
    return lax.all_to_all(value, axes, 0, 0, tiled=True)


def copies(value, count):
    return jnp.broadcast_to(value[None], (count, *value.shape))


def add_bf16(a, b):
    return (a.astype(jnp.float32) + b.astype(jnp.float32)).astype(jnp.bfloat16)


def dot_f32(a, b):
    return jnp.dot(a, b, preferred_element_type=jnp.float32)


def dot_last(a, b):
    return lax.dot_general(a, b, CONTRACT_LAST, preferred_element_type=jnp.float32)


def dot_first(a, b):
    return lax.dot_general(a, b, CONTRACT_FIRST, preferred_element_type=jnp.float32)


def plane_sum(parts, line):
    plane = parts.shape[0] // line
    blocks = exchange(parts.reshape(plane, line, parts.shape[1]), PLANE)
    return jnp.sum(blocks.astype(jnp.float32), axis=0).astype(jnp.bfloat16)


def line_sum(block):
    blocks = exchange(copies(block, lax.axis_size(LINE)), LINE)
    return jnp.sum(blocks.reshape(-1, *block.shape).astype(jnp.float32), axis=0)


def line_sum_steps(block):
    line = lax.axis_size(LINE)
    total = block.astype(jnp.float32)
    stride = 1
    while stride < line:
        pairs = [(i, i ^ stride) for i in range(line)]
        block = total.astype(jnp.bfloat16)
        total = block.astype(jnp.float32) + lax.ppermute(block, LINE, pairs).astype(jnp.float32)
        stride *= 2
    return total


def plane_spread(block, plane):
    return exchange(copies(block, plane), PLANE).reshape(-1, block.shape[1])


def across(value, pairs):
    return lax.ppermute(value, "segment", pairs)


def per_device(
    inputs,
    cotangent,
    gate_weight,
    up_weight,
    down_weight,
    route_rows,
    route_count,
    route_weight,
    width_mask,
):
    width = inputs.shape[2]
    half = width // 2
    line = lax.axis_size(LINE)
    plane = lax.axis_size("x") * lax.axis_size("y")
    tokens = plane * line
    first = lax.axis_index("segment") == 0
    gate_w = gate_weight[0]
    up_w = up_weight[0]
    down_w = down_weight[0]
    keep = width_mask[0, 0].astype(jnp.float32)
    to_one, to_zero, both = [(0, 1)], [(1, 0)], [(0, 1), (1, 0)]

    slots = route_rows.shape[2]
    live = jnp.arange(slots, dtype=jnp.int32) < route_count[0, 0]
    slot_scale = jnp.where(live, route_weight[0, 0], 0.0)
    chosen = route_rows[0, 0][None, :] == jnp.arange(tokens, dtype=jnp.int32)[:, None]
    scale = jnp.sum(jnp.where(chosen, slot_scale[None, :], 0.0), axis=1, keepdims=True)

    def expert_inputs(low, high):
        gate_value = dot_f32(low, gate_w[:half]) + dot_f32(high, gate_w[half:])
        up_value = dot_f32(low, up_w[:half]) + dot_f32(high, up_w[half:])
        return gate_value, up_value

    def scaled(rows):
        return (scale * rows.astype(jnp.float32)).astype(jnp.bfloat16)

    def hidden_of(gate_value, up_value):
        return (gate_value * jax.nn.sigmoid(gate_value) * up_value * keep).astype(jnp.bfloat16)

    def slot_gradient(gate_delta, up_delta, columns):
        return (
            dot_last(gate_delta, gate_w[columns]) + dot_last(up_delta, up_w[columns])
        ).astype(jnp.bfloat16)

    in_row = inputs[0].reshape(2, half // LANES, LANES)
    in_half = jnp.where(first, in_row[0], in_row[1])
    cot_row = cotangent[0].reshape(width // LANES, LANES)
    rows = jnp.concatenate([in_half, cot_row], axis=0)
    rows = exchange(copies(rows, line), LINE)
    in_block = rows[:, : half // LANES].reshape(line, half)
    cot_block = rows[:, half // LANES :].reshape(line, width)
    cot_half = jnp.where(first, cot_block[:, :half], cot_block[:, half:])

    in_mine = plane_spread(in_block, plane)
    in_other = across(in_mine, to_zero)
    gate_zero, up_zero = expert_inputs(in_mine, in_other)
    hidden = hidden_of(gate_zero, up_zero)
    out_high = (scale * dot_f32(hidden, down_w[:, half:])).astype(jnp.bfloat16)
    received = across(out_high, to_one)
    out_low = (scale * dot_f32(hidden, down_w[:, :half])).astype(jnp.bfloat16)
    partial = jnp.where(first, out_low, received)
    partial, cot_part = lax.optimization_barrier((plane_sum(partial, line), cot_half))
    cot_mine = plane_spread(cot_part, plane)
    mid_block = add_bf16(in_block, line_sum_steps(partial))
    mid_block, cot_mine = lax.optimization_barrier((mid_block, cot_mine))
    cot_other = across(cot_mine, to_one)
    mid_mine = plane_spread(mid_block, plane)
    mid_other = across(mid_mine, to_one)

    cot_low, cot_high = scaled(cot_other), scaled(cot_mine)
    delta_one = dot_last(cot_low, down_w[:, :half]) + dot_last(cot_high, down_w[:, half:])
    gate_one, up_one = expert_inputs(mid_other, mid_mine)
    gate_value = jnp.where(first, gate_zero, gate_one)
    up_value = jnp.where(first, up_zero, up_one)
    sig = jax.nn.sigmoid(gate_value)
    gate_slope = keep * up_value * sig * (1.0 + gate_value * (1.0 - sig))
    up_slope = keep * gate_value * sig
    gate_delta = (delta_one * gate_slope).astype(jnp.bfloat16)
    up_delta = (delta_one * up_slope).astype(jnp.bfloat16)
    low, high = slice(0, half), slice(half, width)
    grad_low = slot_gradient(gate_delta, up_delta, low)
    received = across(grad_low, to_zero)
    grad_high = slot_gradient(gate_delta, up_delta, high)
    total = line_sum(plane_sum(jnp.where(first, received, grad_high), line))
    back_block = add_bf16(cot_half, total)
    hidden = hidden_of(gate_value, up_value)
    outcome = (scale * dot_f32(hidden, down_w)).astype(jnp.bfloat16)
    back_mine = plane_spread(back_block, plane)
    back_other = across(back_mine, to_zero)

    back_low, back_high = scaled(back_mine), scaled(back_other)
    delta_zero = dot_last(back_low, down_w[:, :half]) + dot_last(back_high, down_w[:, half:])
    delta = jnp.where(first, delta_zero, delta_one)
    gate_delta = (delta * gate_slope).astype(jnp.bfloat16)
    up_delta = (delta * up_slope).astype(jnp.bfloat16)
    slot_grad = slot_gradient(gate_delta, up_delta, slice(0, width))
    block = plane_sum(jnp.where(first, slot_grad, outcome), line)
    parts = exchange(block.reshape(line, width // LANES, LANES), LINE)
    total = jnp.sum(parts.astype(jnp.float32), axis=0).reshape(width)

    place = lax.axis_index(LINE)
    mine = jnp.stack([mid_block, back_block], axis=1)[place]
    other = across(mine, both)
    whole = jnp.concatenate(
        [jnp.where(first, mine, other), jnp.where(first, other, mine)], axis=1
    )
    mid_row, back_row = whole[0], whole[1]
    last = (jnp.where(first, back_row, mid_row).astype(jnp.float32) + total).astype(jnp.bfloat16)
    section_output = jnp.where(first, mid_row, last)
    grad_input = jnp.where(first, last, back_row)

    picked_low = jnp.where(first, in_mine, mid_other)
    picked_high = jnp.where(first, in_other, mid_mine)
    picked = jnp.concatenate([picked_low, picked_high], axis=1)
    slot_low = jnp.where(first, back_low, cot_low)
    slot_high = jnp.where(first, back_high, cot_high)
    slot_grad_in = jnp.concatenate([slot_low, slot_high], axis=1)
    grad_gate = dot_first(picked, gate_delta)
    grad_up = dot_first(picked, up_delta)
    grad_down = dot_first(hidden, slot_grad_in)
    return (
        section_output.reshape(1, 1, 1, width),
        grad_input.reshape(1, 1, 1, width),
        grad_gate.astype(jnp.bfloat16)[None],
        grad_up.astype(jnp.bfloat16)[None],
        grad_down.astype(jnp.bfloat16)[None],
    )


def solution(mesh):
    torus = Mesh(mesh.devices.reshape(-1, *SIZES), ("segment", *ET))
    return jax.shard_map(
        per_device,
        mesh=torus,
        in_specs=(
            P(None, ET, None),
            P(None, ET, None),
            P("segment", None, ET),
            P("segment", None, ET),
            P("segment", ET, None),
            P("segment", None, None),
            P("segment", None),
            P("segment", None, None),
            P("segment", ET),
        ),
        out_specs=(
            P("segment", None, ET, None),
            P("segment", None, ET, None),
            P("segment", None, ET),
            P("segment", None, ET),
            P("segment", ET, None),
        ),
        check_vma=False,
    )
```

```python
import jax
import jax.numpy as jnp
from jax import lax
from jax.sharding import Mesh
from jax.sharding import PartitionSpec as P

LANES = 128
PLANE = ("x", "y")
LINE = "z"
ET = ("x", "y", "z")
SIZES = (4, 4, 8)
CONTRACT_LAST = (((1,), (1,)), ((), ()))
CONTRACT_FIRST = (((0,), (0,)), ((), ()))


def exchange(value, axes):
    return lax.all_to_all(value, axes, 0, 0, tiled=True)


def copies(value, count):
    return jnp.broadcast_to(value[None], (count, *value.shape))


def add_bf16(a, b):
    return (a.astype(jnp.float32) + b.astype(jnp.float32)).astype(jnp.bfloat16)


def dot_f32(a, b):
    return jnp.dot(a, b, preferred_element_type=jnp.float32)


def dot_last(a, b):
    return lax.dot_general(a, b, CONTRACT_LAST, preferred_element_type=jnp.float32)


def dot_first(a, b):
    return lax.dot_general(a, b, CONTRACT_FIRST, preferred_element_type=jnp.float32)


def plane_sum(parts, line):
    plane = parts.shape[0] // line
    blocks = exchange(parts.reshape(plane, line, parts.shape[1]), PLANE)
    return jnp.sum(blocks.astype(jnp.float32), axis=0).astype(jnp.bfloat16)


def line_sum_steps(block):
    line = lax.axis_size(LINE)
    total = block.astype(jnp.float32)
    stride = 1
    while stride < line:
        pairs = [(i, i ^ stride) for i in range(line)]
        block = total.astype(jnp.bfloat16)
        total = block.astype(jnp.float32) + lax.ppermute(block, LINE, pairs).astype(jnp.float32)
        stride *= 2
    return total


def plane_spread(block, plane):
    return exchange(copies(block, plane), PLANE).reshape(-1, block.shape[1])


def swap(value):
    return lax.ppermute(value, "segment", [(0, 1), (1, 0)])


def per_device(
    inputs,
    cotangent,
    gate_weight,
    up_weight,
    down_weight,
    route_rows,
    route_count,
    route_weight,
    width_mask,
):
    width = inputs.shape[2]
    half = width // 2
    units = gate_weight.shape[2]
    line = lax.axis_size(LINE)
    plane = lax.axis_size("x") * lax.axis_size("y")
    tokens = plane * line
    first = lax.axis_index("segment") == 0

    def pick(a, b):
        return jnp.where(first, a, b)

    def by_section(own):
        other = swap(own)
        return pick(own, other), pick(other, own)

    slots = route_rows.shape[2]
    live = jnp.arange(slots, dtype=jnp.int32) < route_count[0, 0]
    slot_scale = jnp.where(live, route_weight[0, 0], 0.0)
    chosen = route_rows[0, 0][None, :] == jnp.arange(tokens, dtype=jnp.int32)[:, None]
    scale = jnp.sum(jnp.where(chosen, slot_scale[None, :], 0.0), axis=1)
    keep = jnp.broadcast_to(width_mask[0, 0].astype(jnp.float32), (tokens,))
    small = by_section(jnp.stack([scale, keep]))
    scales = [part[0][:, None] for part in small]
    keeps = [part[1][:, None] for part in small]

    def halves(own, axis):
        low = lax.slice_in_dim(own, 0, half, axis=axis)
        high = lax.slice_in_dim(own, half, width, axis=axis)
        mine, other = pick(low, high), swap(pick(high, low))
        return pick(mine, other), pick(other, mine)

    ins = halves(jnp.concatenate([gate_weight[0], up_weight[0]], axis=1), 0)
    downs = halves(down_weight[0], 1)

    def scaled(rows, section):
        return (scales[section] * rows.astype(jnp.float32)).astype(jnp.bfloat16)

    def total_of(part):
        return part + swap(part)

    def forward(rows, section):
        both = total_of(dot_f32(rows, ins[section]))
        gate_value, up_value = both[:, :units], both[:, units:]
        sig = jax.nn.sigmoid(gate_value)
        hidden = (gate_value * sig * up_value * keeps[section]).astype(jnp.bfloat16)
        gate_slope = keeps[section] * up_value * sig * (1.0 + gate_value * (1.0 - sig))
        up_slope = keeps[section] * gate_value * sig
        return hidden, jnp.concatenate([gate_slope, up_slope], axis=1)

    def outcome(hidden, section):
        return (scales[section] * dot_f32(hidden, downs[section])).astype(jnp.bfloat16)

    def hidden_delta(rows, section):
        return total_of(dot_last(rows, downs[section]))

    def deltas_of(delta, slopes):
        return (jnp.concatenate([delta, delta], axis=1) * slopes).astype(jnp.bfloat16)

    def slot_gradient(deltas, section):
        return dot_last(deltas, ins[section]).astype(jnp.bfloat16)

    parts = half // LANES
    in_row = inputs[0].reshape(2, parts, LANES)
    cot_row = cotangent[0].reshape(2, parts, LANES)
    rows = jnp.concatenate([pick(in_row[0], in_row[1]), pick(cot_row[0], cot_row[1])], axis=0)
    rows = exchange(copies(rows, line), LINE)
    in_block = rows[:, :parts].reshape(line, half)
    cot_block = rows[:, parts:].reshape(line, half)

    in_rows = plane_spread(in_block, plane)
    hidden_zero, slopes_zero = forward(in_rows, 0)
    partial = plane_sum(outcome(hidden_zero, 0), line)
    partial, cot_part = lax.optimization_barrier((partial, cot_block))
    cot_rows = plane_spread(cot_part, plane)
    mid_block = add_bf16(in_block, line_sum_steps(partial))
    mid_block, cot_rows = lax.optimization_barrier((mid_block, cot_rows))
    mid_rows = plane_spread(mid_block, plane)

    cot_scaled = scaled(cot_rows, 1)
    delta_one = hidden_delta(cot_scaled, 1)
    hidden_one, slopes_one = forward(mid_rows, 1)
    deltas_one = deltas_of(delta_one, slopes_one)
    partial = plane_sum(slot_gradient(deltas_one, 1), line)
    outcome_one = outcome(hidden_one, 1)
    partial, outcome_one = lax.optimization_barrier((partial, outcome_one))
    out_partial = plane_sum(outcome_one, line)
    back_block = add_bf16(cot_block, line_sum_steps(partial))
    back_block, out_partial = lax.optimization_barrier((back_block, out_partial))
    back_rows = plane_spread(back_block, plane)

    back_scaled = scaled(back_rows, 0)
    deltas_zero = deltas_of(hidden_delta(back_scaled, 0), slopes_zero)
    partial = plane_sum(slot_gradient(deltas_zero, 0), line)
    ends = jnp.stack(
        [partial.reshape(line, parts, LANES), out_partial.reshape(line, parts, LANES)], axis=1
    )
    ends = jnp.sum(exchange(ends, LINE).astype(jnp.float32), axis=0)

    place = lax.axis_index(LINE)
    mid_row = mid_block[place].reshape(parts, LANES)
    back_row = back_block[place].reshape(parts, LANES)
    early = swap(pick(back_row, mid_row))
    last_grad = add_bf16(back_row, ends[0])
    last_out = add_bf16(mid_row, ends[1])
    late = swap(pick(last_out, last_grad))
    section_output = jnp.concatenate([pick(mid_row, late), pick(early, last_out)], axis=0)
    grad_input = jnp.concatenate([pick(last_grad, early), pick(late, back_row)], axis=0)

    other = swap(pick(mid_rows, in_rows))
    picked = jnp.concatenate([pick(in_rows, other), pick(other, mid_rows)], axis=1)
    other = swap(pick(cot_scaled, back_scaled))
    slot_grad_in = jnp.concatenate([pick(back_scaled, other), pick(other, cot_scaled)], axis=1)
    deltas = pick(deltas_zero, deltas_one)
    grad_gate = dot_first(picked, deltas[:, :units])
    grad_up = dot_first(picked, deltas[:, units:])
    grad_down = dot_first(pick(hidden_zero, hidden_one), slot_grad_in)
    return (
        section_output.reshape(1, 1, 1, width),
        grad_input.reshape(1, 1, 1, width),
        grad_gate.astype(jnp.bfloat16)[None],
        grad_up.astype(jnp.bfloat16)[None],
        grad_down.astype(jnp.bfloat16)[None],
    )


def solution(mesh):
    torus = Mesh(mesh.devices.reshape(-1, *SIZES), ("segment", *ET))
    return jax.shard_map(
        per_device,
        mesh=torus,
        in_specs=(
            P(None, ET, None),
            P(None, ET, None),
            P("segment", None, ET),
            P("segment", None, ET),
            P("segment", ET, None),
            P("segment", None, None),
            P("segment", None),
            P("segment", None, None),
            P("segment", ET),
        ),
        out_specs=(
            P("segment", None, ET, None),
            P("segment", None, ET, None),
            P("segment", None, ET),
            P("segment", None, ET),
            P("segment", ET, None),
        ),
        check_vma=False,
    )
```

```python
import jax
import jax.numpy as jnp
from jax import lax
from jax.sharding import Mesh
from jax.sharding import PartitionSpec as P

LANES = 128
PLANE = ("x", "y")
LINE = "z"
ET = ("x", "y", "z")
SIZES = (4, 4, 8)
CONTRACT_LAST = (((1,), (1,)), ((), ()))
CONTRACT_FIRST = (((0,), (0,)), ((), ()))


def exchange(value, axes):
    return lax.all_to_all(value, axes, 0, 0, tiled=True)


def copies(value, count):
    return jnp.broadcast_to(value[None], (count, *value.shape))


def add_bf16(a, b):
    return (a.astype(jnp.float32) + b.astype(jnp.float32)).astype(jnp.bfloat16)


def dot_f32(a, b):
    return jnp.dot(a, b, preferred_element_type=jnp.float32)


def dot_last(a, b):
    return lax.dot_general(a, b, CONTRACT_LAST, preferred_element_type=jnp.float32)


def dot_first(a, b):
    return lax.dot_general(a, b, CONTRACT_FIRST, preferred_element_type=jnp.float32)


def plane_sum(parts, line):
    plane = parts.shape[0] // line
    blocks = exchange(parts.reshape(plane, line, parts.shape[1]), PLANE)
    return jnp.sum(blocks.astype(jnp.float32), axis=0).astype(jnp.bfloat16)


def line_sum(block):
    blocks = exchange(copies(block, lax.axis_size(LINE)), LINE)
    return jnp.sum(blocks.reshape(-1, *block.shape).astype(jnp.float32), axis=0)


def line_sum_steps(block):
    line = lax.axis_size(LINE)
    total = block.astype(jnp.float32)
    stride = 1
    while stride < line:
        pairs = [(i, i ^ stride) for i in range(line)]
        block = total.astype(jnp.bfloat16)
        total = block.astype(jnp.float32) + lax.ppermute(block, LINE, pairs).astype(jnp.float32)
        stride *= 2
    return total


def plane_spread(block, plane):
    return exchange(copies(block, plane), PLANE).reshape(-1, block.shape[1])


def swap(value):
    return lax.ppermute(value, "segment", [(0, 1), (1, 0)])


def per_device(
    inputs,
    cotangent,
    gate_weight,
    up_weight,
    down_weight,
    route_rows,
    route_count,
    route_weight,
    width_mask,
):
    width = inputs.shape[2]
    half = width // 2
    units = gate_weight.shape[2]
    line = lax.axis_size(LINE)
    plane = lax.axis_size("x") * lax.axis_size("y")
    tokens = plane * line
    first = lax.axis_index("segment") == 0

    def pick(a, b):
        return jnp.where(first, a, b)

    def by_section(own):
        other = swap(own)
        return pick(own, other), pick(other, own)

    slots = route_rows.shape[2]
    live = jnp.arange(slots, dtype=jnp.int32) < route_count[0, 0]
    slot_scale = jnp.where(live, route_weight[0, 0], 0.0)
    chosen = route_rows[0, 0][None, :] == jnp.arange(tokens, dtype=jnp.int32)[:, None]
    scale = jnp.sum(jnp.where(chosen, slot_scale[None, :], 0.0), axis=1)
    keep = jnp.broadcast_to(width_mask[0, 0].astype(jnp.float32), (tokens,))
    small = by_section(jnp.stack([scale, keep]))
    scales = [part[0][:, None] for part in small]
    keeps = [part[1][:, None] for part in small]

    def halves(own, axis):
        low = lax.slice_in_dim(own, 0, half, axis=axis)
        high = lax.slice_in_dim(own, half, width, axis=axis)
        mine, other = pick(low, high), swap(pick(high, low))
        return pick(mine, other), pick(other, mine)

    ins = halves(jnp.concatenate([gate_weight[0], up_weight[0]], axis=1), 0)
    downs = halves(down_weight[0], 1)

    def scaled(rows, section):
        return (scales[section] * rows.astype(jnp.float32)).astype(jnp.bfloat16)

    def total_of(part):
        return part + swap(part)

    def forward(rows, section):
        both = total_of(dot_f32(rows, ins[section]))
        gate_value, up_value = both[:, :units], both[:, units:]
        sig = jax.nn.sigmoid(gate_value)
        hidden = (gate_value * sig * up_value * keeps[section]).astype(jnp.bfloat16)
        gate_slope = keeps[section] * up_value * sig * (1.0 + gate_value * (1.0 - sig))
        up_slope = keeps[section] * gate_value * sig
        return hidden, jnp.concatenate([gate_slope, up_slope], axis=1)

    def outcome(hidden, section):
        return (scales[section] * dot_f32(hidden, downs[section])).astype(jnp.bfloat16)

    def hidden_delta(rows, section):
        return total_of(dot_last(rows, downs[section]))

    def deltas_of(delta, slopes):
        return (jnp.concatenate([delta, delta], axis=1) * slopes).astype(jnp.bfloat16)

    def slot_gradient(deltas, section):
        return dot_last(deltas, ins[section]).astype(jnp.bfloat16)

    parts = half // LANES
    in_row = inputs[0].reshape(2, parts, LANES)
    cot_row = cotangent[0].reshape(2, parts, LANES)
    rows = jnp.concatenate([pick(in_row[0], in_row[1]), pick(cot_row[0], cot_row[1])], axis=0)
    rows = exchange(copies(rows, line), LINE)
    in_block = rows[:, :parts].reshape(line, half)
    cot_block = rows[:, parts:].reshape(line, half)

    in_rows = plane_spread(in_block, plane)
    hidden_zero, slopes_zero = forward(in_rows, 0)
    partial = plane_sum(outcome(hidden_zero, 0), line)
    partial, cot_part = lax.optimization_barrier((partial, cot_block))
    cot_rows = plane_spread(cot_part, plane)
    mid_block = add_bf16(in_block, line_sum_steps(partial))
    mid_block, cot_rows = lax.optimization_barrier((mid_block, cot_rows))
    mid_rows = plane_spread(mid_block, plane)

    cot_scaled = scaled(cot_rows, 1)
    delta_one = hidden_delta(cot_scaled, 1)
    hidden_one, slopes_one = forward(mid_rows, 1)
    deltas_one = deltas_of(delta_one, slopes_one)
    partial = plane_sum(slot_gradient(deltas_one, 1), line)
    outcome_one = outcome(hidden_one, 1)
    out_partial = lax.psum_scatter(outcome_one, "x", scatter_dimension=0, tiled=True)
    back_block = add_bf16(cot_block, line_sum(partial))
    back_block, out_partial = lax.optimization_barrier((back_block, out_partial))
    out_partial = lax.psum_scatter(out_partial, "y", scatter_dimension=0, tiled=True)
    back_rows = plane_spread(back_block, plane)

    back_scaled = scaled(back_rows, 0)
    deltas_zero = deltas_of(hidden_delta(back_scaled, 0), slopes_zero)
    shared = swap(pick(mid_rows, in_rows))
    grad_zero, shared, back_scaled, mid_block, back_block = lax.optimization_barrier(
        (slot_gradient(deltas_zero, 0), shared, back_scaled, mid_block, back_block)
    )
    partial, out_partial = lax.optimization_barrier((plane_sum(grad_zero, line), out_partial))
    ends = jnp.stack(
        [partial.reshape(line, parts, LANES), out_partial.reshape(line, parts, LANES)], axis=1
    )
    ends = jnp.sum(exchange(ends, LINE).astype(jnp.float32), axis=0)

    place = lax.axis_index(LINE)
    mid_row = mid_block[place].reshape(parts, LANES)
    back_row = back_block[place].reshape(parts, LANES)
    early = swap(pick(back_row, mid_row))
    last_grad = add_bf16(back_row, ends[0])
    last_out = add_bf16(mid_row, ends[1])
    late = swap(pick(last_out, last_grad))
    section_output = jnp.concatenate([pick(mid_row, late), pick(early, last_out)], axis=0)
    grad_input = jnp.concatenate([pick(last_grad, early), pick(late, back_row)], axis=0)

    picked = jnp.concatenate([pick(in_rows, shared), pick(shared, mid_rows)], axis=1)
    other = swap(pick(cot_scaled, back_scaled))
    slot_grad_in = jnp.concatenate([pick(back_scaled, other), pick(other, cot_scaled)], axis=1)
    deltas = pick(deltas_zero, deltas_one)
    grad_gate = dot_first(picked, deltas[:, :units])
    grad_up = dot_first(picked, deltas[:, units:])
    grad_down = dot_first(pick(hidden_zero, hidden_one), slot_grad_in)
    return (
        section_output.reshape(1, 1, 1, width),
        grad_input.reshape(1, 1, 1, width),
        grad_gate.astype(jnp.bfloat16)[None],
        grad_up.astype(jnp.bfloat16)[None],
        grad_down.astype(jnp.bfloat16)[None],
    )


def solution(mesh):
    torus = Mesh(mesh.devices.reshape(-1, *SIZES), ("segment", *ET))
    return jax.shard_map(
        per_device,
        mesh=torus,
        in_specs=(
            P(None, ET, None),
            P(None, ET, None),
            P("segment", None, ET),
            P("segment", None, ET),
            P("segment", ET, None),
            P("segment", None, None),
            P("segment", None),
            P("segment", None, None),
            P("segment", ET),
        ),
        out_specs=(
            P("segment", None, ET, None),
            P("segment", None, ET, None),
            P("segment", None, ET),
            P("segment", None, ET),
            P("segment", ET, None),
        ),
        check_vma=False,
    )
```

```python
import jax
import jax.numpy as jnp
from jax import lax
from jax.sharding import Mesh
from jax.sharding import PartitionSpec as P

LANES = 128
PLANE = ("x", "y")
LINE = "z"
ET = ("x", "y", "z")
SIZES = (4, 4, 8)
CONTRACT_LAST = (((1,), (1,)), ((), ()))
CONTRACT_FIRST = (((0,), (0,)), ((), ()))


def exchange(value, axes):
    return lax.all_to_all(value, axes, 0, 0, tiled=True)


def copies(value, count):
    return jnp.broadcast_to(value[None], (count, *value.shape))


def add_bf16(a, b):
    return (a.astype(jnp.float32) + b.astype(jnp.float32)).astype(jnp.bfloat16)


def dot_f32(a, b):
    return jnp.dot(a, b, preferred_element_type=jnp.float32)


def dot_last(a, b):
    return lax.dot_general(a, b, CONTRACT_LAST, preferred_element_type=jnp.float32)


def dot_first(a, b):
    return lax.dot_general(a, b, CONTRACT_FIRST, preferred_element_type=jnp.float32)


def plane_sum(parts, line):
    plane = parts.shape[0] // line
    blocks = exchange(parts.reshape(plane, line, parts.shape[1]), PLANE)
    return jnp.sum(blocks.astype(jnp.float32), axis=0).astype(jnp.bfloat16)


def line_sum_steps(block):
    line = lax.axis_size(LINE)
    total = block.astype(jnp.float32)
    stride = 1
    while stride < line:
        pairs = [(i, i ^ stride) for i in range(line)]
        block = total.astype(jnp.bfloat16)
        total = block.astype(jnp.float32) + lax.ppermute(block, LINE, pairs).astype(jnp.float32)
        stride *= 2
    return total


def plane_spread(block, plane):
    return exchange(copies(block, plane), PLANE).reshape(-1, block.shape[1])


def swap(value):
    return lax.ppermute(value, "segment", [(0, 1), (1, 0)])


def per_device(
    inputs,
    cotangent,
    gate_weight,
    up_weight,
    down_weight,
    route_rows,
    route_count,
    route_weight,
    width_mask,
):
    width = inputs.shape[2]
    half = width // 2
    units = gate_weight.shape[2]
    line = lax.axis_size(LINE)
    plane = lax.axis_size("x") * lax.axis_size("y")
    tokens = plane * line
    first = lax.axis_index("segment") == 0

    def pick(a, b):
        return jnp.where(first, a, b)

    slots = route_rows.shape[2]
    live = jnp.arange(slots, dtype=jnp.int32) < route_count[0, 0]
    slot_scale = jnp.where(live, route_weight[0, 0], 0.0)
    chosen = route_rows[0, 0][None, :] == jnp.arange(tokens, dtype=jnp.int32)[:, None]
    scale = jnp.sum(jnp.where(chosen, slot_scale[None, :], 0.0), axis=1)
    keep = jnp.broadcast_to(width_mask[0, 0].astype(jnp.float32), (tokens,))
    own = jnp.stack([scale, keep])
    other = swap(own)
    small = pick(own, other), pick(other, own)
    scales = [part[0][:, None] for part in small]
    keeps = [part[1][:, None] for part in small]

    def halves(own, axis):
        low = lax.slice_in_dim(own, 0, half, axis=axis)
        high = lax.slice_in_dim(own, half, width, axis=axis)
        mine, other = pick(low, high), swap(pick(high, low))
        return pick(mine, other), pick(other, mine)

    ins = halves(jnp.concatenate([gate_weight[0], up_weight[0]], axis=1), 0)
    downs = halves(down_weight[0], 1)

    def scaled(rows, section):
        return (scales[section] * rows.astype(jnp.float32)).astype(jnp.bfloat16)

    def total_of(part):
        return part + swap(part)

    def forward(rows, section):
        both = total_of(dot_f32(rows, ins[section]))
        gate_value, up_value = both[:, :units], both[:, units:]
        sig = jax.nn.sigmoid(gate_value)
        hidden = (gate_value * sig * up_value * keeps[section]).astype(jnp.bfloat16)
        gate_slope = keeps[section] * up_value * sig * (1.0 + gate_value * (1.0 - sig))
        up_slope = keeps[section] * gate_value * sig
        return hidden, jnp.concatenate([gate_slope, up_slope], axis=1)

    def outcome(hidden, section):
        return (scales[section] * dot_f32(hidden, downs[section])).astype(jnp.bfloat16)

    def hidden_delta(rows, section):
        return total_of(dot_last(rows, downs[section]))

    def deltas_of(delta, slopes):
        return (jnp.concatenate([delta, delta], axis=1) * slopes).astype(jnp.bfloat16)

    def slot_gradient(deltas, section):
        return dot_last(deltas, ins[section]).astype(jnp.bfloat16)

    parts = half // LANES
    in_row = inputs[0].reshape(2, parts, LANES)
    cot_row = cotangent[0].reshape(2, parts, LANES)
    rows = jnp.concatenate([pick(in_row[0], in_row[1]), pick(cot_row[0], cot_row[1])], axis=0)
    rows = exchange(copies(rows, line), LINE)
    in_block = rows[:, :parts].reshape(line, half)
    cot_block = rows[:, parts:].reshape(line, half)

    in_rows = plane_spread(in_block, plane)
    hidden_zero, slopes_zero = forward(in_rows, 0)
    partial = plane_sum(outcome(hidden_zero, 0), line)
    partial, cot_part = lax.optimization_barrier((partial, cot_block))
    cot_rows = plane_spread(cot_part, plane)
    mid_block = add_bf16(in_block, line_sum_steps(partial))
    mid_block, cot_rows = lax.optimization_barrier((mid_block, cot_rows))
    mid_rows = plane_spread(mid_block, plane)

    cot_scaled = scaled(cot_rows, 1)
    delta_one = hidden_delta(cot_scaled, 1)
    mid_rows, delta_one = lax.optimization_barrier((mid_rows, delta_one))
    hidden_one, slopes_one = forward(mid_rows, 1)
    deltas_one = deltas_of(delta_one, slopes_one)
    partial = plane_sum(slot_gradient(deltas_one, 1), line)
    outcome_one = outcome(hidden_one, 1)
    partial, outcome_one = lax.optimization_barrier((partial, outcome_one))
    out_partial = plane_sum(outcome_one, line)
    back_block = add_bf16(cot_block, line_sum_steps(partial))
    back_block, out_partial = lax.optimization_barrier((back_block, out_partial))
    back_rows = plane_spread(back_block, plane)

    back_scaled = scaled(back_rows, 0)
    deltas_zero = deltas_of(hidden_delta(back_scaled, 0), slopes_zero)
    partial = plane_sum(slot_gradient(deltas_zero, 0), line)
    ends = jnp.concatenate([partial, out_partial], axis=0).reshape(-1, parts, LANES)
    ends = exchange(ends, ("segment", LINE)).reshape(2, line, parts, LANES)
    ends = jnp.sum(ends.astype(jnp.float32), axis=1).reshape(2 * parts, LANES)

    place = lax.axis_index(LINE)
    own = jnp.stack([mid_block[place], back_block[place]]).reshape(2, parts, LANES)
    other = swap(own)
    mid_row, back_row = jnp.concatenate([pick(own, other), pick(other, own)], axis=1)
    last = (pick(back_row, mid_row).astype(jnp.float32) + ends).astype(jnp.bfloat16)
    section_output = pick(mid_row, last)
    grad_input = pick(last, back_row)

    other = swap(pick(mid_rows, in_rows))
    picked = jnp.concatenate([pick(in_rows, other), pick(other, mid_rows)], axis=1)
    other = swap(pick(cot_scaled, back_scaled))
    slot_grad_in = jnp.concatenate([pick(back_scaled, other), pick(other, cot_scaled)], axis=1)
    deltas = pick(deltas_zero, deltas_one)
    grad_gate = dot_first(picked, deltas[:, :units])
    grad_up = dot_first(picked, deltas[:, units:])
    grad_down = dot_first(pick(hidden_zero, hidden_one), slot_grad_in)
    return (
        section_output.reshape(1, 1, 1, width),
        grad_input.reshape(1, 1, 1, width),
        grad_gate.astype(jnp.bfloat16)[None],
        grad_up.astype(jnp.bfloat16)[None],
        grad_down.astype(jnp.bfloat16)[None],
    )


def solution(mesh):
    torus = Mesh(mesh.devices.reshape(-1, *SIZES), ("segment", *ET))
    return jax.shard_map(
        per_device,
        mesh=torus,
        in_specs=(
            P(None, ET, None),
            P(None, ET, None),
            P("segment", None, ET),
            P("segment", None, ET),
            P("segment", ET, None),
            P("segment", None, None),
            P("segment", None),
            P("segment", None, None),
            P("segment", ET),
        ),
        out_specs=(
            P("segment", None, ET, None),
            P("segment", None, ET, None),
            P("segment", None, ET),
            P("segment", None, ET),
            P("segment", ET, None),
        ),
        check_vma=False,
    )
```

```python
import jax
import jax.numpy as jnp
from jax import lax
from jax.sharding import Mesh
from jax.sharding import PartitionSpec as P

LANES = 128
PLANE = ("x", "y")
LINE = "z"
ET = ("x", "y", "z")
SIZES = (4, 4, 8)
CONTRACT_LAST = (((1,), (1,)), ((), ()))
CONTRACT_FIRST = (((0,), (0,)), ((), ()))


def exchange(value, axes):
    return lax.all_to_all(value, axes, 0, 0, tiled=True)


def copies(value, count):
    return jnp.broadcast_to(value[None], (count, *value.shape))


def add_bf16(a, b):
    return (a.astype(jnp.float32) + b.astype(jnp.float32)).astype(jnp.bfloat16)


def dot_f32(a, b):
    return jnp.dot(a, b, preferred_element_type=jnp.float32)


def dot_last(a, b):
    return lax.dot_general(a, b, CONTRACT_LAST, preferred_element_type=jnp.float32)


def dot_first(a, b):
    return lax.dot_general(a, b, CONTRACT_FIRST, preferred_element_type=jnp.float32)


def plane_sum(parts, line):
    plane = parts.shape[0] // line
    blocks = exchange(parts.reshape(plane, line, parts.shape[1]), PLANE)
    return jnp.sum(blocks.astype(jnp.float32), axis=0).astype(jnp.bfloat16)


def line_sum(block):
    blocks = exchange(copies(block, lax.axis_size(LINE)), LINE)
    return jnp.sum(blocks.reshape(-1, *block.shape).astype(jnp.float32), axis=0)


def plane_spread(block, plane):
    return exchange(copies(block, plane), PLANE).reshape(-1, block.shape[1])


def across(value, pairs):
    return lax.ppermute(value, "segment", pairs)


def swap(value):
    return across(value, [(0, 1), (1, 0)])


def per_device(
    inputs,
    cotangent,
    gate_weight,
    up_weight,
    down_weight,
    route_rows,
    route_count,
    route_weight,
    width_mask,
):
    width = inputs.shape[2]
    half = width // 2
    units = gate_weight.shape[2]
    line = lax.axis_size(LINE)
    plane = lax.axis_size("x") * lax.axis_size("y")
    tokens = plane * line
    first = lax.axis_index("segment") == 0

    def pick(a, b):
        return jnp.where(first, a, b)

    slots = route_rows.shape[2]
    live = jnp.arange(slots, dtype=jnp.int32) < route_count[0, 0]
    slot_scale = jnp.where(live, route_weight[0, 0], 0.0)
    chosen = route_rows[0, 0][None, :] == jnp.arange(tokens, dtype=jnp.int32)[:, None]
    scale = jnp.sum(jnp.where(chosen, slot_scale[None, :], 0.0), axis=1)
    keep = jnp.broadcast_to(width_mask[0, 0].astype(jnp.float32), (tokens,))
    own = jnp.stack([scale, keep])
    other = swap(own)
    small = pick(own, other), pick(other, own)
    scales = [part[0][:, None] for part in small]
    keeps = [part[1][:, None] for part in small]

    def halves(own, axis):
        low = lax.slice_in_dim(own, 0, half, axis=axis)
        high = lax.slice_in_dim(own, half, width, axis=axis)
        mine, other = pick(low, high), swap(pick(high, low))
        return pick(mine, other), pick(other, mine)

    ins = halves(jnp.concatenate([gate_weight[0], up_weight[0]], axis=1), 0)
    downs = halves(down_weight[0], 1)

    def scaled(rows, section):
        return (scales[section] * rows.astype(jnp.float32)).astype(jnp.bfloat16)

    def total_of(part):
        return part + swap(part)

    def forward(rows, section):
        both = total_of(dot_f32(rows, ins[section]))
        gate_value, up_value = both[:, :units], both[:, units:]
        sig = jax.nn.sigmoid(gate_value)
        hidden = (gate_value * sig * up_value * keeps[section]).astype(jnp.bfloat16)
        gate_slope = keeps[section] * up_value * sig * (1.0 + gate_value * (1.0 - sig))
        up_slope = keeps[section] * gate_value * sig
        return hidden, jnp.concatenate([gate_slope, up_slope], axis=1)

    def outcome(hidden, section):
        return (scales[section] * dot_f32(hidden, downs[section])).astype(jnp.bfloat16)

    def hidden_delta(rows, section):
        return total_of(dot_last(rows, downs[section]))

    def deltas_of(delta, slopes):
        return (jnp.concatenate([delta, delta], axis=1) * slopes).astype(jnp.bfloat16)

    def slot_gradient(deltas, section):
        return dot_last(deltas, ins[section]).astype(jnp.bfloat16)

    parts = half // LANES
    in_row = inputs[0].reshape(2, parts, LANES)
    cot_row = cotangent[0].reshape(2, parts, LANES)
    rows = jnp.concatenate([pick(in_row[0], in_row[1]), pick(cot_row[0], cot_row[1])], axis=0)
    rows = exchange(copies(rows, line), LINE)
    in_block = rows[:, :parts].reshape(line, half)
    cot_block = rows[:, parts:].reshape(line, half)

    all_rows = plane_spread(jnp.concatenate([in_block, cot_block], axis=1), plane)
    in_rows, cot_rows = all_rows[:, :half], all_rows[:, half:]
    hidden_zero, slopes_zero = forward(in_rows, 0)
    partial = plane_sum(outcome(hidden_zero, 0), line)
    mid_block = add_bf16(in_block, line_sum(partial))
    mid_rows = plane_spread(mid_block, plane)

    cot_scaled = scaled(cot_rows, 1)
    delta_one = hidden_delta(cot_scaled, 1)
    mid_rows, delta_one = lax.optimization_barrier((mid_rows, delta_one))
    hidden_one, slopes_one = forward(mid_rows, 1)
    deltas_one = deltas_of(delta_one, slopes_one)
    partial = plane_sum(slot_gradient(deltas_one, 1), line)
    outcome_one = outcome(hidden_one, 1)
    back_block = add_bf16(cot_block, line_sum(partial))
    back_rows = plane_spread(back_block, plane)

    in_other, mid_other = across(in_rows, [(1, 0)]), across(mid_rows, [(0, 1)])
    cot_other = across(cot_scaled, [(0, 1)])
    back_scaled = scaled(back_rows, 0)
    back_other = across(back_scaled, [(1, 0)])
    deltas_zero = deltas_of(hidden_delta(back_scaled, 0), slopes_zero)
    grad_zero, in_other, mid_other, cot_other = lax.optimization_barrier(
        (slot_gradient(deltas_zero, 0), in_other, mid_other, cot_other)
    )
    ends = plane_sum(jnp.concatenate([grad_zero, outcome_one], axis=1), line)
    ends = ends.reshape(line, 2, parts, LANES).swapaxes(0, 1).reshape(-1, parts, LANES)
    ends = exchange(ends, ("segment", LINE)).reshape(2, line, parts, LANES)
    ends = jnp.sum(ends.astype(jnp.float32), axis=1).reshape(2 * parts, LANES)

    place = lax.axis_index(LINE)
    own = jnp.stack([mid_block[place], back_block[place]]).reshape(2, parts, LANES)
    other = swap(own)
    mid_row, back_row = jnp.concatenate([pick(own, other), pick(other, own)], axis=1)
    last = (pick(back_row, mid_row).astype(jnp.float32) + ends).astype(jnp.bfloat16)
    section_output = pick(mid_row, last)
    grad_input = pick(last, back_row)

    picked = jnp.concatenate([pick(in_rows, mid_other), pick(in_other, mid_rows)], axis=1)
    slot_grad_in = jnp.concatenate(
        [pick(back_scaled, cot_other), pick(back_other, cot_scaled)], axis=1
    )
    deltas = pick(deltas_zero, deltas_one)
    grad_gate = dot_first(picked, deltas[:, :units])
    grad_up = dot_first(picked, deltas[:, units:])
    grad_down = dot_first(pick(hidden_zero, hidden_one), slot_grad_in)
    return (
        section_output.reshape(1, 1, 1, width),
        grad_input.reshape(1, 1, 1, width),
        grad_gate.astype(jnp.bfloat16)[None],
        grad_up.astype(jnp.bfloat16)[None],
        grad_down.astype(jnp.bfloat16)[None],
    )


def solution(mesh):
    torus = Mesh(mesh.devices.reshape(-1, *SIZES), ("segment", *ET))
    return jax.shard_map(
        per_device,
        mesh=torus,
        in_specs=(
            P(None, ET, None),
            P(None, ET, None),
            P("segment", None, ET),
            P("segment", None, ET),
            P("segment", ET, None),
            P("segment", None, None),
            P("segment", None),
            P("segment", None, None),
            P("segment", ET),
        ),
        out_specs=(
            P("segment", None, ET, None),
            P("segment", None, ET, None),
            P("segment", None, ET),
            P("segment", None, ET),
            P("segment", ET, None),
        ),
        check_vma=False,
    )
```

```python
import jax
import jax.numpy as jnp
from jax import lax
from jax.sharding import Mesh
from jax.sharding import PartitionSpec as P

LANES = 128
PLANE = ("x", "y")
LINE = "z"
ET = ("x", "y", "z")
SIZES = (4, 4, 8)
CONTRACT_LAST = (((1,), (1,)), ((), ()))
CONTRACT_FIRST = (((0,), (0,)), ((), ()))


def exchange(value, axes):
    return lax.all_to_all(value, axes, 0, 0, tiled=True)


def copies(value, count):
    return jnp.broadcast_to(value[None], (count, *value.shape))


def add_bf16(a, b):
    return (a.astype(jnp.float32) + b.astype(jnp.float32)).astype(jnp.bfloat16)


def dot_f32(a, b):
    return jnp.dot(a, b, preferred_element_type=jnp.float32)


def dot_last(a, b):
    return lax.dot_general(a, b, CONTRACT_LAST, preferred_element_type=jnp.float32)


def dot_first(a, b):
    return lax.dot_general(a, b, CONTRACT_FIRST, preferred_element_type=jnp.float32)


def plane_sum(parts, line):
    plane = parts.shape[0] // line
    blocks = exchange(parts.reshape(plane, line, parts.shape[1]), PLANE)
    return jnp.sum(blocks.astype(jnp.float32), axis=0).astype(jnp.bfloat16)


def line_sum_steps(block):
    line = lax.axis_size(LINE)
    total = block.astype(jnp.float32)
    stride = 1
    while stride < line:
        pairs = [(i, i ^ stride) for i in range(line)]
        block = total.astype(jnp.bfloat16)
        total = block.astype(jnp.float32) + lax.ppermute(block, LINE, pairs).astype(jnp.float32)
        stride *= 2
    return total


def plane_spread(block, plane):
    return exchange(copies(block, plane), PLANE).reshape(-1, block.shape[1])


def across(value, pairs):
    return lax.ppermute(value, "segment", pairs)


def swap(value):
    return across(value, [(0, 1), (1, 0)])


def per_device(
    inputs,
    cotangent,
    gate_weight,
    up_weight,
    down_weight,
    route_rows,
    route_count,
    route_weight,
    width_mask,
):
    width = inputs.shape[2]
    half = width // 2
    units = gate_weight.shape[2]
    line = lax.axis_size(LINE)
    plane = lax.axis_size("x") * lax.axis_size("y")
    tokens = plane * line
    first = lax.axis_index("segment") == 0

    def pick(a, b):
        return jnp.where(first, a, b)

    slots = route_rows.shape[2]
    live = jnp.arange(slots, dtype=jnp.int32) < route_count[0, 0]
    slot_scale = jnp.where(live, route_weight[0, 0], 0.0)
    chosen = route_rows[0, 0][None, :] == jnp.arange(tokens, dtype=jnp.int32)[:, None]
    scale = jnp.sum(jnp.where(chosen, slot_scale[None, :], 0.0), axis=1)
    keep = jnp.broadcast_to(width_mask[0, 0].astype(jnp.float32), (tokens,))
    own = jnp.stack([scale, keep])
    other = swap(own)
    small = pick(own, other), pick(other, own)
    scales = [part[0][:, None] for part in small]
    keeps = [part[1][:, None] for part in small]

    def halves(own, axis):
        low = lax.slice_in_dim(own, 0, half, axis=axis)
        high = lax.slice_in_dim(own, half, width, axis=axis)
        mine, other = pick(low, high), swap(pick(high, low))
        return pick(mine, other), pick(other, mine)

    ins = halves(jnp.concatenate([gate_weight[0], up_weight[0]], axis=1), 0)
    downs = halves(down_weight[0], 1)

    def scaled(rows, section):
        return (scales[section] * rows.astype(jnp.float32)).astype(jnp.bfloat16)

    def total_of(part):
        return part + swap(part)

    def forward(rows, section):
        both = total_of(dot_f32(rows, ins[section]))
        gate_value, up_value = both[:, :units], both[:, units:]
        sig = jax.nn.sigmoid(gate_value)
        hidden = (gate_value * sig * up_value * keeps[section]).astype(jnp.bfloat16)
        gate_slope = keeps[section] * up_value * sig * (1.0 + gate_value * (1.0 - sig))
        up_slope = keeps[section] * gate_value * sig
        return hidden, jnp.concatenate([gate_slope, up_slope], axis=1)

    def outcome(hidden, section):
        return (scales[section] * dot_f32(hidden, downs[section])).astype(jnp.bfloat16)

    def hidden_delta(rows, section):
        return total_of(dot_last(rows, downs[section]))

    def deltas_of(delta, slopes):
        return (jnp.concatenate([delta, delta], axis=1) * slopes).astype(jnp.bfloat16)

    def slot_gradient(deltas, section):
        return dot_last(deltas, ins[section]).astype(jnp.bfloat16)

    parts = half // LANES
    in_row = inputs[0].reshape(2, parts, LANES)
    cot_row = cotangent[0].reshape(2, parts, LANES)
    rows = jnp.concatenate([pick(in_row[0], in_row[1]), pick(cot_row[0], cot_row[1])], axis=0)
    rows = exchange(copies(rows, line), LINE)
    in_block = rows[:, :parts].reshape(line, half)
    cot_block = rows[:, parts:].reshape(line, half)

    in_rows = plane_spread(in_block, plane)
    hidden_zero, slopes_zero = forward(in_rows, 0)
    partial = plane_sum(outcome(hidden_zero, 0), line)
    partial, cot_part = lax.optimization_barrier((partial, cot_block))
    cot_rows = plane_spread(cot_part, plane)
    mid_block = add_bf16(in_block, line_sum_steps(partial))
    mid_block, cot_rows = lax.optimization_barrier((mid_block, cot_rows))
    mid_rows = plane_spread(mid_block, plane)

    cot_scaled = scaled(cot_rows, 1)
    delta_one = hidden_delta(cot_scaled, 1)
    mid_rows, delta_one = lax.optimization_barrier((mid_rows, delta_one))
    hidden_one, slopes_one = forward(mid_rows, 1)
    deltas_one = deltas_of(delta_one, slopes_one)
    partial = plane_sum(slot_gradient(deltas_one, 1), line)
    outcome_one = outcome(hidden_one, 1)
    partial, outcome_one = lax.optimization_barrier((partial, outcome_one))
    out_partial = plane_sum(outcome_one, line)
    back_block = add_bf16(cot_block, line_sum_steps(partial))
    back_block, out_partial, in_late, mid_late, cot_late, mid_block = lax.optimization_barrier(
        (back_block, out_partial, in_rows, mid_rows, cot_scaled, mid_block)
    )
    back_rows = plane_spread(back_block, plane)
    in_other, mid_other = across(in_late, [(1, 0)]), across(mid_late, [(0, 1)])
    cot_other = across(cot_late, [(0, 1)])

    back_scaled = scaled(back_rows, 0)
    deltas_zero = deltas_of(hidden_delta(back_scaled, 0), slopes_zero)
    back_other = across(back_scaled, [(1, 0)])
    grad_zero, in_other, mid_other, cot_other = lax.optimization_barrier(
        (slot_gradient(deltas_zero, 0), in_other, mid_other, cot_other)
    )
    partial = plane_sum(grad_zero, line)
    ends = jnp.concatenate([partial, out_partial], axis=0).reshape(-1, parts, LANES)
    ends = exchange(ends, ("segment", LINE)).reshape(2, line, parts, LANES)
    ends = jnp.sum(ends.astype(jnp.float32), axis=1).reshape(2 * parts, LANES)

    place = lax.axis_index(LINE)
    own = jnp.stack([mid_block[place], back_block[place]]).reshape(2, parts, LANES)
    other = swap(own)
    mid_row, back_row = jnp.concatenate([pick(own, other), pick(other, own)], axis=1)
    last = (pick(back_row, mid_row).astype(jnp.float32) + ends).astype(jnp.bfloat16)
    section_output = pick(mid_row, last)
    grad_input = pick(last, back_row)

    picked = jnp.concatenate([pick(in_rows, mid_other), pick(in_other, mid_rows)], axis=1)
    slot_grad_in = jnp.concatenate(
        [pick(back_scaled, cot_other), pick(back_other, cot_scaled)], axis=1
    )
    deltas = pick(deltas_zero, deltas_one)
    grad_gate = dot_first(picked, deltas[:, :units])
    grad_up = dot_first(picked, deltas[:, units:])
    grad_down = dot_first(pick(hidden_zero, hidden_one), slot_grad_in)
    return (
        section_output.reshape(1, 1, 1, width),
        grad_input.reshape(1, 1, 1, width),
        grad_gate.astype(jnp.bfloat16)[None],
        grad_up.astype(jnp.bfloat16)[None],
        grad_down.astype(jnp.bfloat16)[None],
    )


def solution(mesh):
    torus = Mesh(mesh.devices.reshape(-1, *SIZES), ("segment", *ET))
    return jax.shard_map(
        per_device,
        mesh=torus,
        in_specs=(
            P(None, ET, None),
            P(None, ET, None),
            P("segment", None, ET),
            P("segment", None, ET),
            P("segment", ET, None),
            P("segment", None, None),
            P("segment", None),
            P("segment", None, None),
            P("segment", ET),
        ),
        out_specs=(
            P("segment", None, ET, None),
            P("segment", None, ET, None),
            P("segment", None, ET),
            P("segment", None, ET),
            P("segment", ET, None),
        ),
        check_vma=False,
    )
```

```python
import jax
import jax.numpy as jnp
from jax import lax
from jax.sharding import Mesh
from jax.sharding import PartitionSpec as P

LANES = 128
PLANE = ("x", "y")
LINE = "z"
ET = ("x", "y", "z")
SIZES = (4, 4, 8)
CONTRACT_LAST = (((1,), (1,)), ((), ()))
CONTRACT_FIRST = (((0,), (0,)), ((), ()))


def exchange(value, axes):
    return lax.all_to_all(value, axes, 0, 0, tiled=True)


def copies(value, count):
    return jnp.broadcast_to(value[None], (count, *value.shape))


def add_bf16(a, b):
    return (a.astype(jnp.float32) + b.astype(jnp.float32)).astype(jnp.bfloat16)


def dot_f32(a, b):
    return jnp.dot(a, b, preferred_element_type=jnp.float32)


def dot_last(a, b):
    return lax.dot_general(a, b, CONTRACT_LAST, preferred_element_type=jnp.float32)


def dot_first(a, b):
    return lax.dot_general(a, b, CONTRACT_FIRST, preferred_element_type=jnp.float32)


def plane_sum(parts, line):
    plane = parts.shape[0] // line
    blocks = exchange(parts.reshape(plane, line, parts.shape[1]), PLANE)
    return jnp.sum(blocks.astype(jnp.float32), axis=0).astype(jnp.bfloat16)


def line_sum(block):
    blocks = exchange(copies(block, lax.axis_size(LINE)), LINE)
    return jnp.sum(blocks.reshape(-1, *block.shape).astype(jnp.float32), axis=0)


def line_sum_steps(block):
    line = lax.axis_size(LINE)
    total = block.astype(jnp.float32)
    stride = 1
    while stride < line:
        pairs = [(i, i ^ stride) for i in range(line)]
        block = total.astype(jnp.bfloat16)
        total = block.astype(jnp.float32) + lax.ppermute(block, LINE, pairs).astype(jnp.float32)
        stride *= 2
    return total


def plane_spread(block, plane):
    return exchange(copies(block, plane), PLANE).reshape(-1, block.shape[1])


def across(value, pairs):
    return lax.ppermute(value, "segment", pairs)


def swap(value):
    return across(value, [(0, 1), (1, 0)])


def per_device(
    inputs,
    cotangent,
    gate_weight,
    up_weight,
    down_weight,
    route_rows,
    route_count,
    route_weight,
    width_mask,
):
    width = inputs.shape[2]
    half = width // 2
    units = gate_weight.shape[2]
    line = lax.axis_size(LINE)
    plane = lax.axis_size("x") * lax.axis_size("y")
    tokens = plane * line
    first = lax.axis_index("segment") == 0

    def pick(a, b):
        return jnp.where(first, a, b)

    slots = route_rows.shape[2]
    live = jnp.arange(slots, dtype=jnp.int32) < route_count[0, 0]
    slot_scale = jnp.where(live, route_weight[0, 0], 0.0)
    chosen = route_rows[0, 0][None, :] == jnp.arange(tokens, dtype=jnp.int32)[:, None]
    scale = jnp.sum(jnp.where(chosen, slot_scale[None, :], 0.0), axis=1)
    keep = jnp.broadcast_to(width_mask[0, 0].astype(jnp.float32), (tokens,))
    own = jnp.stack([scale, keep])
    other = swap(own)
    small = pick(own, other), pick(other, own)
    scales = [part[0][:, None] for part in small]
    keeps = [part[1][:, None] for part in small]

    def halves(own, axis):
        low = lax.slice_in_dim(own, 0, half, axis=axis)
        high = lax.slice_in_dim(own, half, width, axis=axis)
        mine, other = pick(low, high), swap(pick(high, low))
        return pick(mine, other), pick(other, mine)

    ins = halves(jnp.concatenate([gate_weight[0], up_weight[0]], axis=1), 0)
    downs = halves(down_weight[0], 1)

    def scaled(rows, section):
        return (scales[section] * rows.astype(jnp.float32)).astype(jnp.bfloat16)

    def total_of(part):
        return part + swap(part)

    def forward(rows, section):
        both = total_of(dot_f32(rows, ins[section]))
        gate_value, up_value = both[:, :units], both[:, units:]
        sig = jax.nn.sigmoid(gate_value)
        hidden = (gate_value * sig * up_value * keeps[section]).astype(jnp.bfloat16)
        gate_slope = keeps[section] * up_value * sig * (1.0 + gate_value * (1.0 - sig))
        up_slope = keeps[section] * gate_value * sig
        return hidden, jnp.concatenate([gate_slope, up_slope], axis=1)

    def outcome(hidden, section):
        return (scales[section] * dot_f32(hidden, downs[section])).astype(jnp.bfloat16)

    def hidden_delta(rows, section):
        return scales[section] * total_of(dot_last(rows, downs[section]))

    def deltas_of(delta, slopes):
        return (jnp.concatenate([delta, delta], axis=1) * slopes).astype(jnp.bfloat16)

    def slot_gradient(deltas, section):
        return dot_last(deltas, ins[section]).astype(jnp.bfloat16)

    parts = half // LANES
    in_row = inputs[0].reshape(2, parts, LANES)
    cot_row = cotangent[0].reshape(2, parts, LANES)
    rows = jnp.concatenate([pick(in_row[0], in_row[1]), pick(cot_row[0], cot_row[1])], axis=0)
    rows = exchange(copies(rows, line), LINE)
    in_block = rows[:, :parts].reshape(line, half)
    cot_block = rows[:, parts:].reshape(line, half)

    in_rows = plane_spread(in_block, plane)
    hidden_zero, slopes_zero = forward(in_rows, 0)
    partial = plane_sum(outcome(hidden_zero, 0), line)
    partial, cot_part = lax.optimization_barrier((partial, cot_block))
    cot_rows = plane_spread(cot_part, plane)
    mid_block = add_bf16(in_block, line_sum_steps(partial))
    mid_block, cot_rows = lax.optimization_barrier((mid_block, cot_rows))
    mid_rows = plane_spread(mid_block, plane)

    cot_scaled = scaled(cot_rows, 1)
    delta_one = hidden_delta(cot_rows, 1)
    mid_rows, delta_one = lax.optimization_barrier((mid_rows, delta_one))
    hidden_one, slopes_one = forward(mid_rows, 1)
    deltas_one = deltas_of(delta_one, slopes_one)
    partial = plane_sum(slot_gradient(deltas_one, 1), line)
    outcome_one = outcome(hidden_one, 1)
    back_block = add_bf16(cot_block, line_sum(partial))
    back_block, in_late, mid_late, cot_late, mid_block = lax.optimization_barrier(
        (back_block, in_rows, mid_rows, cot_scaled, mid_block)
    )
    back_rows = plane_spread(back_block, plane)
    in_other, mid_other = across(in_late, [(1, 0)]), across(mid_late, [(0, 1)])
    cot_other = across(cot_late, [(0, 1)])

    deltas_zero = deltas_of(hidden_delta(back_rows, 0), slopes_zero)
    grad_zero, in_other, mid_other, cot_other, back_rows = lax.optimization_barrier(
        (slot_gradient(deltas_zero, 0), in_other, mid_other, cot_other, back_rows)
    )
    back_scaled = scaled(back_rows, 0)
    back_other = across(back_scaled, [(1, 0)])
    ends = plane_sum(jnp.concatenate([grad_zero, outcome_one], axis=1), line)
    ends = ends.reshape(line, 2, parts, LANES).swapaxes(0, 1).reshape(-1, parts, LANES)
    ends = exchange(ends, ("segment", LINE)).reshape(2, line, parts, LANES)
    ends = jnp.sum(ends.astype(jnp.float32), axis=1).reshape(2 * parts, LANES)

    place = lax.axis_index(LINE)
    own = jnp.stack([mid_block[place], back_block[place]]).reshape(2, parts, LANES)
    other = swap(own)
    mid_row, back_row = jnp.concatenate([pick(own, other), pick(other, own)], axis=1)
    last = (pick(back_row, mid_row).astype(jnp.float32) + ends).astype(jnp.bfloat16)
    section_output = pick(mid_row, last)
    grad_input = pick(last, back_row)

    picked = jnp.concatenate([pick(in_rows, mid_other), pick(in_other, mid_rows)], axis=1)
    slot_grad_in = jnp.concatenate(
        [pick(back_scaled, cot_other), pick(back_other, cot_scaled)], axis=1
    )
    deltas = pick(deltas_zero, deltas_one)
    grad_gate = dot_first(picked, deltas[:, :units])
    grad_up = dot_first(picked, deltas[:, units:])
    grad_down = dot_first(pick(hidden_zero, hidden_one), slot_grad_in)
    return (
        section_output.reshape(1, 1, 1, width),
        grad_input.reshape(1, 1, 1, width),
        grad_gate.astype(jnp.bfloat16)[None],
        grad_up.astype(jnp.bfloat16)[None],
        grad_down.astype(jnp.bfloat16)[None],
    )


def solution(mesh):
    torus = Mesh(mesh.devices.reshape(-1, *SIZES), ("segment", *ET))
    return jax.shard_map(
        per_device,
        mesh=torus,
        in_specs=(
            P(None, ET, None),
            P(None, ET, None),
            P("segment", None, ET),
            P("segment", None, ET),
            P("segment", ET, None),
            P("segment", None, None),
            P("segment", None),
            P("segment", None, None),
            P("segment", ET),
        ),
        out_specs=(
            P("segment", None, ET, None),
            P("segment", None, ET, None),
            P("segment", None, ET),
            P("segment", None, ET),
            P("segment", ET, None),
        ),
        check_vma=False,
    )
```

```python
import jax
import jax.numpy as jnp
from jax import lax
from jax.sharding import Mesh
from jax.sharding import PartitionSpec as P

LANES = 128
PLANE = ("x", "y")
LINE = "z"
ET = ("x", "y", "z")
SIZES = (4, 4, 8)
CONTRACT_LAST = (((1,), (1,)), ((), ()))
CONTRACT_FIRST = (((0,), (0,)), ((), ()))


def exchange(value, axes):
    return lax.all_to_all(value, axes, 0, 0, tiled=True)


def copies(value, count):
    return jnp.broadcast_to(value[None], (count, *value.shape))


def add_bf16(a, b):
    return (a.astype(jnp.float32) + b.astype(jnp.float32)).astype(jnp.bfloat16)


def dot_f32(a, b):
    return jnp.dot(a, b, preferred_element_type=jnp.float32)


def dot_last(a, b):
    return lax.dot_general(a, b, CONTRACT_LAST, preferred_element_type=jnp.float32)


def dot_first(a, b):
    return lax.dot_general(a, b, CONTRACT_FIRST, preferred_element_type=jnp.float32)


def plane_sum(parts, line):
    plane = parts.shape[0] // line
    blocks = exchange(parts.reshape(plane, line, parts.shape[1]), PLANE)
    return jnp.sum(blocks.astype(jnp.float32), axis=0).astype(jnp.bfloat16)


def line_sum_steps(block):
    line = lax.axis_size(LINE)
    total = block.astype(jnp.float32)
    stride = 1
    while stride < line:
        pairs = [(i, i ^ stride) for i in range(line)]
        block = total.astype(jnp.bfloat16)
        total = block.astype(jnp.float32) + lax.ppermute(block, LINE, pairs).astype(jnp.float32)
        stride *= 2
    return total


def plane_spread(block, plane):
    return exchange(copies(block, plane), PLANE).reshape(-1, block.shape[1])


def across(value, pairs):
    return lax.ppermute(value, "segment", pairs)


def swap(value):
    return across(value, [(0, 1), (1, 0)])


def per_device(
    inputs,
    cotangent,
    gate_weight,
    up_weight,
    down_weight,
    route_rows,
    route_count,
    route_weight,
    width_mask,
):
    width = inputs.shape[2]
    half = width // 2
    units = gate_weight.shape[2]
    line = lax.axis_size(LINE)
    plane = lax.axis_size("x") * lax.axis_size("y")
    tokens = plane * line
    first = lax.axis_index("segment") == 0

    def pick(a, b):
        return jnp.where(first, a, b)

    slots = route_rows.shape[2]
    live = jnp.arange(slots, dtype=jnp.int32) < route_count[0, 0]
    slot_scale = jnp.where(live, route_weight[0, 0], 0.0)
    chosen = route_rows[0, 0][None, :] == jnp.arange(tokens, dtype=jnp.int32)[:, None]
    scale = jnp.sum(jnp.where(chosen, slot_scale[None, :], 0.0), axis=1)
    keep = jnp.broadcast_to(width_mask[0, 0].astype(jnp.float32), (tokens,))
    own = jnp.stack([scale, keep])
    other = swap(own)
    small = pick(own, other), pick(other, own)
    scales = [part[0][:, None] for part in small]
    keeps = [part[1][:, None] for part in small]

    def halves(own, axis):
        low = lax.slice_in_dim(own, 0, half, axis=axis)
        high = lax.slice_in_dim(own, half, width, axis=axis)
        mine, other = pick(low, high), swap(pick(high, low))
        return pick(mine, other), pick(other, mine)

    ins = halves(jnp.concatenate([gate_weight[0], up_weight[0]], axis=1), 0)
    downs = halves(down_weight[0], 1)

    def scaled(rows, section):
        return (scales[section] * rows.astype(jnp.float32)).astype(jnp.bfloat16)

    def total_of(part):
        return part + swap(part)

    def forward(rows, section):
        both = total_of(dot_f32(rows, ins[section]))
        gate_value, up_value = both[:, :units], both[:, units:]
        sig = jax.nn.sigmoid(gate_value)
        hidden = (gate_value * sig * up_value * keeps[section]).astype(jnp.bfloat16)
        gate_slope = keeps[section] * up_value * sig * (1.0 + gate_value * (1.0 - sig))
        up_slope = keeps[section] * gate_value * sig
        return hidden, jnp.concatenate([gate_slope, up_slope], axis=1)

    def outcome(hidden, section):
        return (scales[section] * dot_f32(hidden, downs[section])).astype(jnp.bfloat16)

    def hidden_delta(rows, section):
        return scales[section] * total_of(dot_last(rows, downs[section]))

    def deltas_of(delta, slopes):
        return (jnp.concatenate([delta, delta], axis=1) * slopes).astype(jnp.bfloat16)

    def slot_gradient(deltas, section):
        return dot_last(deltas, ins[section]).astype(jnp.bfloat16)

    parts = half // LANES
    in_row = inputs[0].reshape(2, parts, LANES)
    cot_row = cotangent[0].reshape(2, parts, LANES)
    rows = jnp.concatenate([pick(in_row[0], in_row[1]), pick(cot_row[0], cot_row[1])], axis=0)
    rows = exchange(copies(rows, line), LINE)
    in_block = rows[:, :parts].reshape(line, half)
    cot_block = rows[:, parts:].reshape(line, half)

    in_rows = plane_spread(in_block, plane)
    hidden_zero, slopes_zero = forward(in_rows, 0)
    partial = plane_sum(outcome(hidden_zero, 0), line)
    partial, cot_part = lax.optimization_barrier((partial, cot_block))
    cot_rows = plane_spread(cot_part, plane)
    mid_block = add_bf16(in_block, line_sum_steps(partial))
    mid_block, cot_rows = lax.optimization_barrier((mid_block, cot_rows))
    mid_rows = plane_spread(mid_block, plane)

    cot_scaled = scaled(cot_rows, 1)
    delta_one = hidden_delta(cot_rows, 1)
    mid_rows, delta_one = lax.optimization_barrier((mid_rows, delta_one))
    hidden_one, slopes_one = forward(mid_rows, 1)
    deltas_one = deltas_of(delta_one, slopes_one)
    partial = plane_sum(slot_gradient(deltas_one, 1), line)
    outcome_one = outcome(hidden_one, 1)
    partial, outcome_one = lax.optimization_barrier((partial, outcome_one))
    out_partial = plane_sum(outcome_one, line)
    back_block = add_bf16(cot_block, line_sum_steps(partial))
    back_block, out_partial, in_late, mid_late, cot_late, mid_block = lax.optimization_barrier(
        (back_block, out_partial, in_rows, mid_rows, cot_scaled, mid_block)
    )
    back_rows = plane_spread(back_block, plane)
    in_other, mid_other = across(in_late, [(1, 0)]), across(mid_late, [(0, 1)])
    cot_other = across(cot_late, [(0, 1)])

    deltas_zero = deltas_of(hidden_delta(back_rows, 0), slopes_zero)
    grad_zero, in_other, mid_other, cot_other, back_rows = lax.optimization_barrier(
        (slot_gradient(deltas_zero, 0), in_other, mid_other, cot_other, back_rows)
    )
    back_scaled = scaled(back_rows, 0)
    back_other = across(back_scaled, [(1, 0)])
    partial = plane_sum(grad_zero, line)
    ends = jnp.concatenate([partial, out_partial], axis=0).reshape(-1, parts, LANES)
    ends = exchange(ends, ("segment", LINE)).reshape(2, line, parts, LANES)
    ends = jnp.sum(ends.astype(jnp.float32), axis=1).reshape(2 * parts, LANES)

    place = lax.axis_index(LINE)
    own = jnp.stack([mid_block[place], back_block[place]]).reshape(2, parts, LANES)
    other = swap(own)
    mid_row, back_row = jnp.concatenate([pick(own, other), pick(other, own)], axis=1)
    last = (pick(back_row, mid_row).astype(jnp.float32) + ends).astype(jnp.bfloat16)
    section_output = pick(mid_row, last)
    grad_input = pick(last, back_row)

    picked = jnp.concatenate([pick(in_rows, mid_other), pick(in_other, mid_rows)], axis=1)
    slot_grad_in = jnp.concatenate(
        [pick(back_scaled, cot_other), pick(back_other, cot_scaled)], axis=1
    )
    deltas = pick(deltas_zero, deltas_one)
    grad_gate = dot_first(picked, deltas[:, :units])
    grad_up = dot_first(picked, deltas[:, units:])
    grad_down = dot_first(pick(hidden_zero, hidden_one), slot_grad_in)
    return (
        section_output.reshape(1, 1, 1, width),
        grad_input.reshape(1, 1, 1, width),
        grad_gate.astype(jnp.bfloat16)[None],
        grad_up.astype(jnp.bfloat16)[None],
        grad_down.astype(jnp.bfloat16)[None],
    )


def solution(mesh):
    torus = Mesh(mesh.devices.reshape(-1, *SIZES), ("segment", *ET))
    return jax.shard_map(
        per_device,
        mesh=torus,
        in_specs=(
            P(None, ET, None),
            P(None, ET, None),
            P("segment", None, ET),
            P("segment", None, ET),
            P("segment", ET, None),
            P("segment", None, None),
            P("segment", None),
            P("segment", None, None),
            P("segment", ET),
        ),
        out_specs=(
            P("segment", None, ET, None),
            P("segment", None, ET, None),
            P("segment", None, ET),
            P("segment", None, ET),
            P("segment", ET, None),
        ),
        check_vma=False,
    )
```

```python
import jax
import jax.numpy as jnp
from jax import lax
from jax.sharding import Mesh
from jax.sharding import PartitionSpec as P

LANES = 128
PLANE = ("x", "y")
LINE = "z"
ET = ("x", "y", "z")
SIZES = (4, 4, 8)
CONTRACT_LAST = (((1,), (1,)), ((), ()))
CONTRACT_FIRST = (((0,), (0,)), ((), ()))


def exchange(value, axes):
    return lax.all_to_all(value, axes, 0, 0, tiled=True)


def copies(value, count):
    return jnp.broadcast_to(value[None], (count, *value.shape))


def add_bf16(a, b):
    return (a.astype(jnp.float32) + b.astype(jnp.float32)).astype(jnp.bfloat16)


def dot_f32(a, b):
    return jnp.dot(a, b, preferred_element_type=jnp.float32)


def dot_last(a, b):
    return lax.dot_general(a, b, CONTRACT_LAST, preferred_element_type=jnp.float32)


def dot_first(a, b):
    return lax.dot_general(a, b, CONTRACT_FIRST, preferred_element_type=jnp.float32)


def plane_sum(parts, line):
    plane = parts.shape[0] // line
    blocks = exchange(parts.reshape(plane, line, parts.shape[1]), PLANE)
    return jnp.sum(blocks.astype(jnp.float32), axis=0).astype(jnp.bfloat16)


def line_sum_steps(block):
    line = lax.axis_size(LINE)
    total = block.astype(jnp.float32)
    stride = 1
    while stride < line:
        pairs = [(i, i ^ stride) for i in range(line)]
        block = total.astype(jnp.bfloat16)
        total = block.astype(jnp.float32) + lax.ppermute(block, LINE, pairs).astype(jnp.float32)
        stride *= 2
    return total


def plane_spread(block, plane):
    return exchange(copies(block, plane), PLANE).reshape(-1, block.shape[1])


def across(value, pairs):
    return lax.ppermute(value, "segment", pairs)


def swap(value):
    return across(value, [(0, 1), (1, 0)])


def per_device(
    inputs,
    cotangent,
    gate_weight,
    up_weight,
    down_weight,
    route_rows,
    route_count,
    route_weight,
    width_mask,
):
    width = inputs.shape[2]
    half = width // 2
    units = gate_weight.shape[2]
    line = lax.axis_size(LINE)
    plane = lax.axis_size("x") * lax.axis_size("y")
    tokens = plane * line
    first = lax.axis_index("segment") == 0

    def pick(a, b):
        return jnp.where(first, a, b)

    slots = route_rows.shape[2]
    live = jnp.arange(slots, dtype=jnp.int32) < route_count[0, 0]
    slot_scale = jnp.where(live, route_weight[0, 0], 0.0)
    chosen = route_rows[0, 0][None, :] == jnp.arange(tokens, dtype=jnp.int32)[:, None]
    scale = jnp.sum(jnp.where(chosen, slot_scale[None, :], 0.0), axis=1)
    keep = jnp.broadcast_to(width_mask[0, 0].astype(jnp.float32), (tokens,))
    own = jnp.stack([scale, keep])
    other = swap(own)
    small = pick(own, other), pick(other, own)
    scales = [part[0][:, None] for part in small]
    keeps = [part[1][:, None] for part in small]

    def halves(own, axis):
        low = lax.slice_in_dim(own, 0, half, axis=axis)
        high = lax.slice_in_dim(own, half, width, axis=axis)
        mine, other = pick(low, high), swap(pick(high, low))
        return pick(mine, other), pick(other, mine)

    ins = halves(jnp.concatenate([gate_weight[0], up_weight[0]], axis=1), 0)
    downs = halves(down_weight[0], 1)

    def scaled(rows, section):
        return (scales[section] * rows.astype(jnp.float32)).astype(jnp.bfloat16)

    def total_of(part):
        return part + swap(part)

    def forward(rows, section):
        both = total_of(dot_f32(rows, ins[section]))
        gate_value, up_value = both[:, :units], both[:, units:]
        sig = jax.nn.sigmoid(gate_value)
        hidden = (gate_value * sig * up_value * keeps[section]).astype(jnp.bfloat16)
        gate_slope = keeps[section] * up_value * sig * (1.0 + gate_value * (1.0 - sig))
        up_slope = keeps[section] * gate_value * sig
        return hidden, jnp.concatenate([gate_slope, up_slope], axis=1)

    def outcome(hidden, section):
        return (scales[section] * dot_f32(hidden, downs[section])).astype(jnp.bfloat16)

    def hidden_delta(rows, section):
        return scales[section] * total_of(dot_last(rows, downs[section]))

    def deltas_of(delta, slopes):
        return (jnp.concatenate([delta, delta], axis=1) * slopes).astype(jnp.bfloat16)

    def slot_gradient(deltas, section):
        return dot_last(deltas, ins[section]).astype(jnp.bfloat16)

    parts = half // LANES
    in_row = inputs[0].reshape(2, parts, LANES)
    cot_row = cotangent[0].reshape(2, parts, LANES)
    rows = jnp.concatenate([pick(in_row[0], in_row[1]), pick(cot_row[0], cot_row[1])], axis=0)
    rows = exchange(copies(rows, line), LINE)
    in_block = rows[:, :parts].reshape(line, half)
    cot_block = rows[:, parts:].reshape(line, half)

    in_rows = plane_spread(in_block, plane)
    hidden_zero, slopes_zero = forward(in_rows, 0)
    partial = plane_sum(outcome(hidden_zero, 0), line)
    partial, cot_part = lax.optimization_barrier((partial, cot_block))
    cot_rows = plane_spread(cot_part, plane)
    mid_block = add_bf16(in_block, line_sum_steps(partial))
    mid_block, cot_rows = lax.optimization_barrier((mid_block, cot_rows))
    mid_rows = plane_spread(mid_block, plane)

    cot_scaled = scaled(cot_rows, 1)
    delta_one = hidden_delta(cot_rows, 1)
    mid_rows, delta_one = lax.optimization_barrier((mid_rows, delta_one))
    hidden_one, slopes_one = forward(mid_rows, 1)
    deltas_one = deltas_of(delta_one, slopes_one)
    partial = plane_sum(slot_gradient(deltas_one, 1), line)
    outcome_one = outcome(hidden_one, 1)
    partial, outcome_one = lax.optimization_barrier((partial, outcome_one))
    out_blocks = exchange(outcome_one.reshape(plane, line, half), PLANE)
    back_block = add_bf16(cot_block, line_sum_steps(partial))
    back_block, out_blocks, in_late, mid_late, cot_late, mid_block = lax.optimization_barrier(
        (back_block, out_blocks, in_rows, mid_rows, cot_scaled, mid_block)
    )
    back_rows = plane_spread(back_block, plane)
    out_partial = jnp.sum(out_blocks.astype(jnp.float32), axis=0).astype(jnp.bfloat16)
    in_other, mid_other = across(in_late, [(1, 0)]), across(mid_late, [(0, 1)])
    cot_other = across(cot_late, [(0, 1)])

    deltas_zero = deltas_of(hidden_delta(back_rows, 0), slopes_zero)
    grad_zero, in_other, mid_other, cot_other, back_rows = lax.optimization_barrier(
        (slot_gradient(deltas_zero, 0), in_other, mid_other, cot_other, back_rows)
    )
    back_scaled = scaled(back_rows, 0)
    back_other = across(back_scaled, [(1, 0)])
    partial = plane_sum(grad_zero, line)
    ends = jnp.concatenate([partial, out_partial], axis=0).reshape(-1, parts, LANES)
    ends = exchange(ends, ("segment", LINE)).reshape(2, line, parts, LANES)
    ends = jnp.sum(ends.astype(jnp.float32), axis=1).reshape(2 * parts, LANES)

    place = lax.axis_index(LINE)
    own = jnp.stack([mid_block[place], back_block[place]]).reshape(2, parts, LANES)
    other = swap(own)
    mid_row, back_row = jnp.concatenate([pick(own, other), pick(other, own)], axis=1)
    last = (pick(back_row, mid_row).astype(jnp.float32) + ends).astype(jnp.bfloat16)
    section_output = pick(mid_row, last)
    grad_input = pick(last, back_row)

    picked = jnp.concatenate([pick(in_rows, mid_other), pick(in_other, mid_rows)], axis=1)
    slot_grad_in = jnp.concatenate(
        [pick(back_scaled, cot_other), pick(back_other, cot_scaled)], axis=1
    )
    deltas = pick(deltas_zero, deltas_one)
    grad_gate = dot_first(picked, deltas[:, :units])
    grad_up = dot_first(picked, deltas[:, units:])
    grad_down = dot_first(pick(hidden_zero, hidden_one), slot_grad_in)
    return (
        section_output.reshape(1, 1, 1, width),
        grad_input.reshape(1, 1, 1, width),
        grad_gate.astype(jnp.bfloat16)[None],
        grad_up.astype(jnp.bfloat16)[None],
        grad_down.astype(jnp.bfloat16)[None],
    )


def solution(mesh):
    torus = Mesh(mesh.devices.reshape(-1, *SIZES), ("segment", *ET))
    return jax.shard_map(
        per_device,
        mesh=torus,
        in_specs=(
            P(None, ET, None),
            P(None, ET, None),
            P("segment", None, ET),
            P("segment", None, ET),
            P("segment", ET, None),
            P("segment", None, None),
            P("segment", None),
            P("segment", None, None),
            P("segment", ET),
        ),
        out_specs=(
            P("segment", None, ET, None),
            P("segment", None, ET, None),
            P("segment", None, ET),
            P("segment", None, ET),
            P("segment", ET, None),
        ),
        check_vma=False,
    )
```
